32 devices in a mesh: groups: 2 (over y), row: 8 (over z, x), col: 2 (over core).
Axes of the slice: x: 2, y: 2, z: 4, core: 2. Of those that a mesh axis runs over, the one named last changes fastest.
Arguments:
- slab: float32 [24576, 512], P(('groups', 'row', 'col')), parts along dimension 0, may hold values from -6 to 6
- predictors: float32 [1024, 256], P(('groups', 'row', 'col')), parts along dimension 0, may hold values from -6 to 6
Outputs:
- covariance: float32 [24576, 12288], P(('groups', 'row'), 'col'), parts along dimension 0
The draws below stay inside these ranges and needn't reach their ends.
There are 2 independent parts, one for each index of `groups`. The reference program is written for one: setup_inputs(seed, part) draws one part's arguments, and reference() takes and returns one part's arrays. A program takes and returns all parts, laid end to end along the dimension named above; each array names one. Nothing has to cross between parts.
All inputs are finite; a program needn't handle non-finite values.
Results may differ from the reference program's by a relative error of at most 0.000078.
Values sent between devices are 32-bit elements; how exact they have to be, the bound alone decides.
No kernel may reach another device: no remote copies, remote signals or barrier semaphores. Data moves between devices by JAX's collectives and lax.ppermute only.
A program may use at most 192 MiB of HBM per device.

```python
import jax
import jax.numpy as jnp
from jax import lax

R = 12288
P_SIZE = 256
SAMPLES = 512


def levels(own_key, dims, pieces, least, top_value):
    loudness = 1.0
    for dim, shards_of in pieces:
        draws = jax.random.uniform(jax.random.fold_in(jax.random.fold_in(own_key, 6), dim), (shards_of,), jnp.float32, least / len(pieces), top_value / len(pieces))
        loudness = loudness * jnp.repeat(jnp.exp(draws), dims[dim] // shards_of).reshape((-1,) + (1,) * (len(dims) - 1 - dim))
    return loudness


def noise(stream_key, shape, deviation, bound, shards=(), dtype=jnp.bfloat16):
    array = jax.random.normal(stream_key, shape, jnp.float32) * deviation
    if len(shards) > 0:
        array = levels(stream_key, shape, shards, -0.22, 0.18) * array
    return jnp.clip(array, min=-bound, max=bound).astype(dtype)


def setup_inputs(seed: int = 0, part: int = 0) -> dict:
    keys = jax.random.split(jax.random.key(seed), 3)
    own_keys = jax.random.split(jax.random.fold_in(keys[2], part), 3)
    return {
        "slab": noise(own_keys[0], (R, SAMPLES), 1.0, 6.0, ((0, 16),), jnp.float32),
        "predictors": noise(own_keys[1], (SAMPLES, P_SIZE), 1.0, 6.0, ((0, 16),), jnp.float32),
    }


def reference(slab, predictors):
    high = lax.Precision.HIGHEST
    gram = jnp.dot(predictors.T, predictors, precision=high)
    cross = jnp.dot(predictors.T, slab.T, precision=high)
    coef = jnp.linalg.solve(gram, cross)
    outer = jnp.dot(slab, slab.T, precision=high)
    corr = jnp.dot(cross.T, coef, precision=high)
    return (outer - corr) / jnp.float32(SAMPLES)
```

```python
import functools

import jax
import jax.numpy as jnp
import numpy as np
from jax import lax
from jax.experimental import pallas as pl
from jax.experimental.pallas import tpu as pltpu
from jax.sharding import PartitionSpec as P


f32, bf16 = jnp.float32, jnp.bfloat16
AXES = ("row", "col")
NN = (((1,), (0,)), ((), ()))
TN = (((0,), (0,)), ((), ()))
NT = (((1,), (1,)), ((), ()))
TT = (((0,), (1,)), ((), ()))


def low(a, b, dims=NN):
    return lax.dot_general(a.astype(bf16), b.astype(bf16), dims, preferred_element_type=f32)


def halves(a):
    h = a.astype(bf16)
    return h, (a - h.astype(f32)).astype(bf16)


def mid(a, b, dims=NN):
    ah, al = halves(a)
    bh, bl = halves(b)
    dot = functools.partial(lax.dot_general, dimension_numbers=dims, preferred_element_type=f32)
    return dot(ah, bh) + (dot(ah, bl) + dot(al, bh))


def high(a, b, dims=NN):
    return lax.dot_general(a, b, dims, precision=lax.Precision.HIGHEST, preferred_element_type=f32)


def eye(n):
    r = lax.broadcasted_iota(jnp.int32, (n, n), 0)
    c = lax.broadcasted_iota(jnp.int32, (n, n), 1)
    return jnp.where(r == c, 1.0, 0.0).astype(f32)


def basis_kernel(count, spots, *refs):
    parts, (c_ref, x_ref, g_ref, v_ref, b_ref, z_ref, s_ref, e_ref) = refs[:count], refs[count:]
    m, n = x_ref.shape
    blocks, size = parts[0].shape[:2]
    for i, part in enumerate(parts):
        for j in range(blocks):
            if count * blocks == 1:
                x_ref[...] = part[j]
            else:
                at = pick(spots[:, i * blocks + j])
                x_ref[pl.ds(pl.multiple_of(at * size, size), size), :] = part[j]
    x = x_ref[...]
    ident = eye(n)
    gram = high(x, x, TN)
    bound = jnp.max(jnp.sum(jnp.abs(gram), axis=0, keepdims=True))
    g = gram / bound
    g_ref[...] = g
    v = 3.4445 * ident - 4.7750 * g + 2.0315 * low(g, g)
    k = low(v, low(g, v))
    v = 3.4445 * v - low(v, 4.7750 * k - 2.0315 * low(k, k))
    for _ in range(2):
        k = ident - low(v, low(g, v))
        v = v + low(v, 0.5 * k + 0.375 * low(k, k))
    v_ref[...] = v

    def polish(dot=high):
        v = v_ref[...]
        k = ident - dot(v, dot(g_ref[...], v), TN)
        k2 = low(k, k)
        v_ref[...] = v + mid(v, 0.5 * k + 0.375 * k2 + 0.3125 * low(k, k2))
        return jnp.max(jnp.abs(k))

    polish(mid)
    lax.while_loop(
        lambda at: jnp.logical_and(at[0] < 60, jnp.logical_not(at[1] < 1e-4)),
        lambda at: (at[0] + 1, polish()),
        (jnp.int32(0), polish()),
    )
    v = v_ref[...] * lax.rsqrt(bound)
    v_ref[...] = v
    q1 = high(x, v)
    a = q1[:n]
    s = jnp.where(jnp.sum(a * ident, axis=0, keepdims=True) < 0, 1.0, -1.0).astype(f32)
    s_ref[...] = s
    p = low(v, x[:n], TT) * s
    b_ref[...] = ident - high(v, x[:n], TT) * s
    z = ident + p
    for _ in range(4):
        p = low(p, p)
        z = z + low(z, p)
    z_ref[...] = z

    def refine(dot=high):
        z = z_ref[...]
        k = ident - dot(b_ref[...], z)
        z_ref[...] = z + mid(z, k + low(k, k))
        return jnp.max(jnp.abs(k))

    refine(mid)
    error = refine()

    @pl.when(jnp.logical_not(error < 3e-5))
    def _():
        e_ref[...] = high(x_ref[:n], v_ref[...])
        rows = lax.broadcasted_iota(jnp.int32, (n, n), 0)
        cols = lax.broadcasted_iota(jnp.int32, (n, n), 1)
        lane = lax.broadcasted_iota(jnp.int32, (1, n), 1)

        def step(j, s):
            e = e_ref[...]
            row = jnp.sum(jnp.where(rows == j, e, 0.0), axis=0, keepdims=True)
            col = jnp.sum(jnp.where(cols == j, e, 0.0), axis=1, keepdims=True)
            head = jnp.sum(jnp.where(lane == j, row, 0.0), axis=1, keepdims=True)
            sign = jnp.where(head < 0, 1.0, -1.0)
            col = jnp.where(rows[:, :1] > j, col / (head - sign), 0.0)
            e_ref[...] = e - col * jnp.where(lane == j, row - sign, row)
            return jnp.where(lane == j, sign, s)

        s = lax.fori_loop(0, n, step, jnp.zeros((1, n), f32))
        s_ref[...] = s
        b = eye(n) - high(v_ref[...], x_ref[:n], TT) * s
        b_ref[...] = b
        z_ref[...] = 0.49 * b.T
        lax.while_loop(
            lambda at: jnp.logical_and(at[0] < 60, jnp.logical_not(at[1] < 3e-5)),
            lambda at: (at[0] + 1, refine()),
            (jnp.int32(0), refine()),
        )
        refine()

    q2 = q1[n:]
    nt = -high(q2, z_ref[...], NT)
    c_ref[:, :n] = high(nt, a - ident * s_ref[...], NT)
    c_ref[:, n:] = eye(m - n) + high(nt, q2, NT)


def basis(parts, spots):
    blocks, size, n = parts[0].shape
    m = len(parts) * blocks * size
    return pl.pallas_call(
        functools.partial(basis_kernel, len(parts), spots),
        out_shape=jax.ShapeDtypeStruct((m - n, m), f32),
        in_specs=[pl.BlockSpec(memory_space=pltpu.VMEM)] * len(parts),
        out_specs=pl.BlockSpec(memory_space=pltpu.VMEM),
        scratch_shapes=[pltpu.VMEM((m, n), f32)]
        + [pltpu.VMEM((n, n), f32)] * 4
        + [pltpu.VMEM((1, n), f32), pltpu.VMEM((n, n), f32)],
        compiler_params=pltpu.CompilerParams(vmem_limit_bytes=24 << 20),
        cost_estimate=pl.CostEstimate(flops=8_000_000_000, bytes_accessed=1 << 20, transcendentals=0),
        name="basis",
    )(*parts)


def pick(column):
    device = lax.axis_index("row") * lax.axis_size("col") + lax.axis_index("col")
    value = jnp.int32(int(column[0]))
    for d in range(1, len(column)):
        if column[d] != column[0]:
            value = jnp.where(device == d, jnp.int32(int(column[d])), value)
    return value


def beside(*parts):
    return jnp.concatenate(parts, axis=1)


def project_kernel(count, c_ref, *refs):
    pieces, outs, (held, sem) = refs[:count], refs[count:2 * count], refs[2 * count:]
    for i in range(count):
        pltpu.make_async_copy(pieces[i], held.at[i], sem.at[i]).start()
    ch, cl = halves(c_ref[...])
    cat = beside(ch, cl, ch)
    for i in range(count):
        pltpu.make_async_copy(pieces[i], held.at[i], sem.at[i]).wait()
        h, l = halves(held[i])
        outs[i][...] = lax.dot_general(cat, beside(h, h, l), NT, preferred_element_type=f32)


def project(comp, pieces):
    count = len(pieces)
    shard, samples = pieces[0].shape
    k = comp.shape[0]
    return pl.pallas_call(
        functools.partial(project_kernel, count),
        out_shape=[jax.ShapeDtypeStruct((k, shard), f32)] * count,
        in_specs=[pl.BlockSpec(memory_space=pltpu.VMEM)] + [pl.BlockSpec(memory_space=pltpu.HBM)] * count,
        out_specs=[pl.BlockSpec(memory_space=pltpu.VMEM)] * count,
        scratch_shapes=[pltpu.VMEM((count, shard, samples), f32), pltpu.SemaphoreType.DMA((count,))],
        compiler_params=pltpu.CompilerParams(vmem_limit_bytes=24 << 20),
        cost_estimate=pl.CostEstimate(
            flops=6 * count * shard * samples * k, bytes_accessed=4 * count * shard * (samples + k), transcendentals=0
        ),
        name="project",
    )(comp, *pieces)


def own_kernel(c_ref, mine_ref, theirs_ref, rows_ref, b_ref, held, sem):
    core = lax.axis_index("col")
    shard, samples = held.shape[1:]
    for i, ref in enumerate((mine_ref, theirs_ref)):
        pltpu.make_async_copy(ref, held.at[i], sem.at[i]).start()
    ch, cl = halves(c_ref[...])
    left, right = beside(ch, cl, ch), beside(ch, ch, cl)
    for i, ref in enumerate((mine_ref, theirs_ref)):
        pltpu.make_async_copy(ref, held.at[i], sem.at[i]).wait()
        h, l = halves(held[i])
        if i == 1:
            b_ref[...] = lax.dot_general(left, beside(h, h, l), NT, preferred_element_type=f32)
        w = lax.dot_general(beside(h, l, h), right, NT, preferred_element_type=f32) * (1.0 / samples)
        h, l = halves(w)
        at = pl.ds(pl.multiple_of((core if i == 0 else 1 - core) * shard, shard), shard)
        rows_ref[at, :] = beside(h, l, h)


def own_parts(comp, mine, theirs):
    shard, samples = mine.shape
    k = comp.shape[0]
    return pl.pallas_call(
        own_kernel,
        out_shape=[jax.ShapeDtypeStruct((2 * shard, 3 * k), bf16), jax.ShapeDtypeStruct((k, shard), f32)],
        in_specs=[pl.BlockSpec(memory_space=pltpu.VMEM)] + [pl.BlockSpec(memory_space=pltpu.HBM)] * 2,
        out_specs=[pl.BlockSpec(memory_space=pltpu.VMEM)] * 2,
        scratch_shapes=[pltpu.VMEM((2, shard, samples), f32), pltpu.SemaphoreType.DMA((2,))],
        compiler_params=pltpu.CompilerParams(vmem_limit_bytes=24 << 20),
        cost_estimate=pl.CostEstimate(
            flops=18 * shard * samples * k, bytes_accessed=8 * shard * (samples + 2 * k), transcendentals=0
        ),
        name="own",
    )(comp, mine, theirs)


def tiles_kernel(parts, plan, given, rows_ref, *refs):
    count, turns = sum(parts), plan.shape[1] // 2
    pieces, refs = refs[:count], refs[count + (1 if given else 0):]
    out_ref, held, cat, tile, in_sem, out_sem = refs
    k, shard = held.shape[1:]
    height = tile.shape[2]
    steps = rows_ref.shape[0] // height
    which = [pick(plan[:, 2 * t]) for t in range(turns)]
    slots = [pick(plan[:, 2 * t + 1]) for t in range(turns)]

    def store(turn, t):
        cols = pl.ds(pl.multiple_of(slots[turn] * shard, shard), shard)
        return pltpu.make_async_copy(
            tile.at[turn, t], out_ref.at[pl.ds(t * height, height), cols], out_sem.at[turn, t]
        )

    for turn in range(turns):
        at = 0
        for i, n in enumerate(parts):
            if (plan[:, 2 * turn] == i).any():
                @pl.when(which[turn] == i)
                def _():
                    for j in range(n):
                        into = held.at[turn, pl.ds(j * (k // n), k // n)]
                        pltpu.make_async_copy(pieces[at + j], into, in_sem.at[turn]).start()
            at += n

    for turn in range(turns):
        @pl.when(which[turn] >= 0)
        def _():
            pltpu.make_async_copy(held.at[turn], held.at[turn], in_sem.at[turn]).wait()
            h, l = halves(held[turn])
            cat[:k] = h
            cat[k:2 * k] = h
            cat[2 * k:] = l
            for t in range(steps):
                lhs = rows_ref[t * height:(t + 1) * height, :]
                tile[turn, t] = lax.dot_general(lhs, cat[...], NN, preferred_element_type=f32)
                store(turn, t).start()

    for turn in range(turns):
        @pl.when(which[turn] >= 0)
        def _():
            for t in range(steps):
                store(turn, t).wait()


def tiles(plan, rows, pieces, out, width):
    turns = plan.shape[1] // 2
    k, shard = rows.shape[1] // 3, pieces[0][0].shape[1]
    arrays = [w for piece in pieces for w in piece]
    steps = 3 if rows.shape[0] % 48 == 0 else 2
    height = rows.shape[0] // steps
    given = [] if out is None else [out]
    return pl.pallas_call(
        functools.partial(tiles_kernel, [len(piece) for piece in pieces], plan, out is not None),
        out_shape=jax.ShapeDtypeStruct((rows.shape[0], width), f32),
        in_specs=[pl.BlockSpec(memory_space=pltpu.VMEM)] + [pl.BlockSpec(memory_space=pl.ANY)] * (len(arrays) + len(given)),
        out_specs=pl.BlockSpec(memory_space=pl.ANY),
        scratch_shapes=[
            pltpu.VMEM((turns, k, shard), f32),
            pltpu.VMEM((3 * k, shard), bf16),
            pltpu.VMEM((turns, steps, height, shard), f32),
            pltpu.SemaphoreType.DMA((turns,)),
            pltpu.SemaphoreType.DMA((turns, steps)),
        ],
        input_output_aliases={1 + len(arrays): 0} if given else {},
        compiler_params=pltpu.CompilerParams(vmem_limit_bytes=28 << 20),
        cost_estimate=pl.CostEstimate(
            flops=turns * rows.shape[0] * shard * k * 6, bytes_accessed=turns * rows.shape[0] * shard * 4, transcendentals=0
        ),
        name="tiles",
    )(rows, *arrays, *given)


def gather_all(x, n_row, n_col):
    n = n_row * n_col
    if n & (n - 1) or n_col != 2 or n < 8 or x.shape[0] % 8:
        return [lax.all_gather(x, AXES, axis=0, tiled=True)[None]], np.zeros((n, 1), np.int32)
    y, held = x[None], [0]
    bit = n_col
    while 2 * bit < n:
        other = lax.ppermute(y, AXES, [(i, i ^ bit) for i in range(n)])
        y, held = jnp.concatenate([y, other]), held + [h ^ bit for h in held]
        bit *= 2
    parts, spots = [y], list(held)
    for flip in (bit, 1, bit + 1):
        source = parts[1] if flip == bit + 1 else y
        parts.append(lax.ppermute(source, AXES, [(i, i ^ (1 if flip & 1 else flip)) for i in range(n)]))
        spots += [h ^ flip for h in held]
    return parts, np.array([[i ^ h for h in spots] for i in range(n)], np.int32)


def ring_of(mesh):
    n = mesh.shape["row"]
    at = [getattr(d, "coords", None) for d in mesh.devices[0, :, 0]]
    if any(c is None for c in at):
        return list(range(n))
    axes = [sorted({c[i] for c in at}) for i in range(3)]
    wide = [i for i in range(3) if len(axes[i]) > 1]
    index = {tuple(c): r for r, c in enumerate(at)}
    if len(wide) != 2 or len(index) != n or n != len(axes[wide[0]]) * len(axes[wide[1]]):
        return list(range(n))
    if len(axes[wide[0]]) % 2:
        wide.reverse()
    lines, places = axes[wide[0]], axes[wide[1]]

    def row(line, place):
        c = list(at[0])
        c[wide[0]], c[wide[1]] = line, place
        return index[tuple(c)]

    order = [row(lines[0], places[0])]
    for i, line in enumerate(lines):
        order += [row(line, p) for p in (places[1:] if i % 2 == 0 else places[:0:-1])]
    return order + [row(line, places[0]) for line in lines[:0:-1]]


def shards(ring, slab, predictors):
    return covariance(ring, slab, predictors)


def covariance(ring, slab, predictors):
    n_row, n_col = lax.axis_size("row"), lax.axis_size("col")
    shard, samples = slab.shape
    width = n_row * shard

    if n_col != 2 or n_row % 2 or shard % 128:
        comp = basis(*gather_all(predictors, n_row, n_col))
        w = lax.dot_general(slab, comp, NT, precision=lax.Precision.HIGHEST)
        every = lax.all_gather(w, AXES, axis=0, tiled=True)
        cols = lax.dynamic_slice_in_dim(every, lax.axis_index("col") * width, width)
        rows = lax.dynamic_slice_in_dim(every, lax.axis_index("row") * n_col * shard, n_col * shard)
        return jnp.dot(rows * (1.0 / samples), cols.T, precision=lax.Precision.HIGHEST)

    home = [i * n_col // n_row for i in range(n_row)]
    place = {i: p for p, i in enumerate(ring)}

    def hop(x, way, steps, source=None):
        pairs = []
        for q in range(n_row):
            a, b = ring[(q + way * (steps - 1)) % n_row], ring[(q + way * steps) % n_row]
            h = home[ring[q]]
            pairs.append((a * n_col + (h if source is None else source), b * n_col + h))
        return lax.ppermute(x, AXES, pairs)

    todo = [[[] for _ in range(n_row * n_col)], {}]

    def arrive(offset, core, w):
        key = (offset, core)
        todo[1][key] = w
        for r in range(n_row):
            for c in range(n_col):
                q = ring[(place[r] + offset) % n_row]
                if home[q] == c:
                    e = {"mine": c, "theirs": 1 - c}.get(core, core)
                    todo[0][r * n_col + c].append((key, (q - c * (n_row // n_col)) * n_col + e))

    def work(rows, out, turns=2):
        turns = min(turns, max(len(t) for t in todo[0]))
        if turns == 0:
            return out
        table, names = np.full((n_row * n_col, 2 * turns), -1, np.int32), []
        for d, waiting in enumerate(todo[0]):
            for i in range(min(turns, len(waiting))):
                key, slot = waiting.pop(0)
                if key not in names:
                    names.append(key)
                table[d, 2 * i:2 * i + 2] = names.index(key), slot
        return tiles(table, rows, [todo[1][key] for key in names], out, width)

    half = n_row // 2
    near = {way: hop(slab, way, 1, 0) for way in (1, -1)}
    other = lax.ppermute(slab, "col", [(0, 1), (1, 0)])
    comp = basis(*gather_all(predictors, n_row, n_col))
    (mine,) = project(comp, [slab])
    flights = [(1, 1, {way: hop(mine, way, 1, 1) for way in (1, -1)})]
    first = dict(zip((1, -1), project(comp, [near[1], near[-1]])))

    def onward(core, steps, sent):
        if steps + 1 < half:
            flights.append((core, steps + 1, {way: hop(sent[way], way, steps + 1) for way in sent}))
        elif steps + 1 == half:
            k = sent[1].shape[0] // 2
            flights.append((core, half, {1: hop(sent[1][:k], 1, half), -1: hop(sent[-1][k:], -1, half)}))

    onward(0, 1, first)
    rows, theirs = own_parts(comp, slab, other)
    arrive(0, "mine", [mine])
    arrive(0, "theirs", [theirs])
    for way in (1, -1):
        arrive(-way, 0, [first[way]])
    out = work(rows, None, 1)
    while flights:
        core, steps, sent = flights.pop(0)
        got = lax.optimization_barrier(tuple(sent.values()) + (out,))
        out = got[-1]
        sent = dict(zip(sent, got))
        onward(core, steps, sent)
        if steps < half:
            for way, w in sent.items():
                arrive(-way * steps, core, [w])
        else:
            arrive(half, core, list(sent.values()))
        out = work(rows, out, (1 if steps + 1 < half else 2) if flights else 8)
    return out


def solution(mesh):
    return jax.shard_map(
        functools.partial(shards, ring_of(mesh)),
        mesh=mesh,
        in_specs=(P(("groups", "row", "col"), None), P(("groups", "row", "col"), None)),
        out_specs=P(("groups", "row"), "col"),
        check_vma=False,
    )
```

```python
import functools

import jax
import jax.numpy as jnp
import numpy as np
from jax import lax
from jax.experimental import pallas as pl
from jax.experimental.pallas import tpu as pltpu
from jax.sharding import PartitionSpec as P


f32, bf16 = jnp.float32, jnp.bfloat16
AXES = ("row", "col")
NN = (((1,), (0,)), ((), ()))
TN = (((0,), (0,)), ((), ()))
NT = (((1,), (1,)), ((), ()))


def low(a, b, dims=NN):
    return lax.dot_general(a.astype(bf16), b.astype(bf16), dims, preferred_element_type=f32)


def halves(a):
    h = a.astype(bf16)
    return h, (a - h.astype(f32)).astype(bf16)


def mid(a, b, dims=NN):
    ah, al = halves(a)
    bh, bl = halves(b)
    dot = functools.partial(lax.dot_general, dimension_numbers=dims, preferred_element_type=f32)
    return dot(ah, bh) + (dot(ah, bl) + dot(al, bh))


def high(a, b, dims=NN):
    return lax.dot_general(a, b, dims, precision=lax.Precision.HIGHEST, preferred_element_type=f32)


def eye(n):
    r = lax.broadcasted_iota(jnp.int32, (n, n), 0)
    c = lax.broadcasted_iota(jnp.int32, (n, n), 1)
    return jnp.where(r == c, 1.0, 0.0).astype(f32)


def basis_kernel(count, spots, slab_ref, *refs):
    parts, refs = refs[:count], refs[count:]
    c_ref, w_ref, x_ref, g_ref, v_ref, b_ref, z_ref, s_ref, e_ref, held, sem = refs
    m, n = x_ref.shape
    load = pltpu.make_async_copy(slab_ref, held, sem)
    load.start()
    blocks, size = parts[0].shape[:2]
    for i, part in enumerate(parts):
        for j in range(blocks):
            if count * blocks == 1:
                x_ref[...] = part[j]
            else:
                at = pick(spots[:, i * blocks + j])
                x_ref[pl.ds(pl.multiple_of(at * size, size), size), :] = part[j]
    x = x_ref[...]
    ident = eye(n)
    gram = high(x, x, TN)
    bound = jnp.max(jnp.sum(jnp.abs(gram), axis=0, keepdims=True))
    g = gram / bound
    g_ref[...] = g
    v = 3.4445 * ident - 4.7750 * g + 2.0315 * low(g, g)
    k = low(v, low(g, v))
    v = 3.4445 * v - low(v, 4.7750 * k - 2.0315 * low(k, k))
    for _ in range(2):
        k = ident - low(v, low(g, v))
        v = v + low(v, 0.5 * k + 0.375 * low(k, k))
    v_ref[...] = v

    def polish(k):
        v = v_ref[...]
        k2 = low(k, k)
        v_ref[...] = v + mid(v, 0.5 * k + 0.375 * k2 + 0.3125 * low(k, k2))

    def off(dot=high):
        v = v_ref[...]
        k = ident - dot(v, dot(g_ref[...], v), TN)
        e_ref[...] = k
        return jnp.max(jnp.abs(k))

    def again(at):
        polish(e_ref[...])
        return at[0] + 1, off()

    off(mid)
    polish(e_ref[...])
    lax.while_loop(
        lambda at: jnp.logical_and(at[0] < 60, jnp.logical_not(at[1] < 1e-4)), again, (jnp.int32(0), off())
    )
    v = v_ref[...]
    v = (v + low(v, 0.5 * e_ref[...])) * lax.rsqrt(bound)
    v_ref[...] = v
    q1 = high(x, v)
    a = q1[:n]
    s = jnp.where(jnp.sum(a * ident, axis=0, keepdims=True) < 0, 1.0, -1.0).astype(f32)
    s_ref[...] = s
    p = a.T * s
    b_ref[...] = ident - a.T * s
    z = ident + p
    for _ in range(4):
        p = low(p, p)
        z = z + low(z, p)
    z_ref[...] = z

    def refine(dot=high):
        z = z_ref[...]
        k = ident - dot(b_ref[...], z)
        z_ref[...] = z + mid(z, k + low(k, k))
        return jnp.max(jnp.abs(k))

    refine(mid)
    error = refine()

    @pl.when(jnp.logical_not(error < 3e-5))
    def _():
        e_ref[...] = q1[:n]
        rows = lax.broadcasted_iota(jnp.int32, (n, n), 0)
        cols = lax.broadcasted_iota(jnp.int32, (n, n), 1)
        lane = lax.broadcasted_iota(jnp.int32, (1, n), 1)

        def step(j, s):
            e = e_ref[...]
            row = jnp.sum(jnp.where(rows == j, e, 0.0), axis=0, keepdims=True)
            col = jnp.sum(jnp.where(cols == j, e, 0.0), axis=1, keepdims=True)
            head = jnp.sum(jnp.where(lane == j, row, 0.0), axis=1, keepdims=True)
            sign = jnp.where(head < 0, 1.0, -1.0)
            col = jnp.where(rows[:, :1] > j, col / (head - sign), 0.0)
            e_ref[...] = e - col * jnp.where(lane == j, row - sign, row)
            return jnp.where(lane == j, sign, s)

        s = lax.fori_loop(0, n, step, jnp.zeros((1, n), f32))
        s_ref[...] = s
        b = eye(n) - q1[:n].T * s
        b_ref[...] = b
        z_ref[...] = 0.49 * b.T
        lax.while_loop(
            lambda at: jnp.logical_and(at[0] < 60, jnp.logical_not(at[1] < 3e-5)),
            lambda at: (at[0] + 1, refine()),
            (jnp.int32(0), refine()),
        )
        refine()

    q2 = q1[n:]
    nt = -high(q2, z_ref[...], NT)
    c_ref[:, :n] = high(nt, a - ident * s_ref[...], NT)
    c_ref[:, n:] = eye(m - n) + high(nt, q2, NT)
    load.wait()
    ch, cl = halves(c_ref[...])
    h, l = halves(held[...])
    w_ref[...] = lax.dot_general(beside(ch, cl, ch), beside(h, h, l), NT, preferred_element_type=f32)


def basis(slab, parts, spots):
    blocks, size, n = parts[0].shape
    m = len(parts) * blocks * size
    return pl.pallas_call(
        functools.partial(basis_kernel, len(parts), spots),
        out_shape=[jax.ShapeDtypeStruct((m - n, m), f32), jax.ShapeDtypeStruct((m - n, slab.shape[0]), f32)],
        in_specs=[pl.BlockSpec(memory_space=pl.ANY)] + [pl.BlockSpec(memory_space=pltpu.VMEM)] * len(parts),
        out_specs=[pl.BlockSpec(memory_space=pltpu.VMEM)] * 2,
        scratch_shapes=[pltpu.VMEM((m, n), f32)]
        + [pltpu.VMEM((n, n), f32)] * 4
        + [pltpu.VMEM((1, n), f32), pltpu.VMEM((n, n), f32), pltpu.VMEM(slab.shape, f32), pltpu.SemaphoreType.DMA],
        compiler_params=pltpu.CompilerParams(vmem_limit_bytes=24 << 20),
        cost_estimate=pl.CostEstimate(flops=8_000_000_000, bytes_accessed=1 << 20, transcendentals=0),
        name="basis",
    )(slab, *parts)


def pick(column):
    device = lax.axis_index("row") * lax.axis_size("col") + lax.axis_index("col")
    value = jnp.int32(int(column[0]))
    for d in range(1, len(column)):
        if column[d] != column[0]:
            value = jnp.where(device == d, jnp.int32(int(column[d])), value)
    return value


def beside(*parts):
    return jnp.concatenate(parts, axis=1)


def project_kernel(count, c_ref, *refs):
    pieces, outs, (held, sem) = refs[:count], refs[count:2 * count], refs[2 * count:]
    for i in range(count):
        pltpu.make_async_copy(pieces[i], held.at[i], sem.at[i]).start()
    ch, cl = halves(c_ref[...])
    cat = beside(ch, cl, ch)
    for i in range(count):
        pltpu.make_async_copy(pieces[i], held.at[i], sem.at[i]).wait()
        h, l = halves(held[i])
        outs[i][...] = lax.dot_general(cat, beside(h, h, l), NT, preferred_element_type=f32)


def project(comp, pieces):
    count = len(pieces)
    shard, samples = pieces[0].shape
    k = comp.shape[0]
    return pl.pallas_call(
        functools.partial(project_kernel, count),
        out_shape=[jax.ShapeDtypeStruct((k, shard), f32)] * count,
        in_specs=[pl.BlockSpec(memory_space=pltpu.VMEM)] + [pl.BlockSpec(memory_space=pltpu.HBM)] * count,
        out_specs=[pl.BlockSpec(memory_space=pltpu.VMEM)] * count,
        scratch_shapes=[pltpu.VMEM((count, shard, samples), f32), pltpu.SemaphoreType.DMA((count,))],
        compiler_params=pltpu.CompilerParams(vmem_limit_bytes=24 << 20),
        cost_estimate=pl.CostEstimate(
            flops=6 * count * shard * samples * k, bytes_accessed=4 * count * shard * (samples + k), transcendentals=0
        ),
        name="project",
    )(comp, *pieces)


def own_kernel(samples, c_ref, mine_ref, theirs_ref, rows_ref, b_ref):
    core = lax.axis_index("col")
    shard = mine_ref.shape[1]
    ch, cl = halves(c_ref[...])
    h, l = halves(theirs_ref[...])
    theirs = lax.dot_general(beside(ch, cl, ch), beside(h, h, l), NT, preferred_element_type=f32)
    b_ref[...] = theirs
    for i, w in enumerate((mine_ref[...], theirs)):
        h, l = halves(w.T * (1.0 / samples))
        at = pl.ds(pl.multiple_of((core if i == 0 else 1 - core) * shard, shard), shard)
        rows_ref[at, :] = beside(h, l, h)


def own_parts(comp, mine, theirs):
    shard, samples = theirs.shape
    k = comp.shape[0]
    return pl.pallas_call(
        functools.partial(own_kernel, samples),
        out_shape=[jax.ShapeDtypeStruct((2 * shard, 3 * k), bf16), jax.ShapeDtypeStruct((k, shard), f32)],
        in_specs=[pl.BlockSpec(memory_space=pltpu.VMEM)] * 3,
        out_specs=[pl.BlockSpec(memory_space=pltpu.VMEM)] * 2,
        compiler_params=pltpu.CompilerParams(vmem_limit_bytes=24 << 20),
        cost_estimate=pl.CostEstimate(
            flops=6 * shard * samples * k, bytes_accessed=8 * shard * (samples + 2 * k), transcendentals=0
        ),
        name="own",
    )(comp, mine, theirs)


def tiles_kernel(parts, plan, given, rows_ref, *refs):
    count, turns = sum(parts), plan.shape[1] // 2
    pieces, refs = refs[:count], refs[count + (1 if given else 0):]
    out_ref, held, cat, tile, in_sem, out_sem = refs
    k, shard = held.shape[1:]
    height = tile.shape[2]
    steps = rows_ref.shape[0] // height
    which = [pick(plan[:, 2 * t]) for t in range(turns)]
    slots = [pick(plan[:, 2 * t + 1]) for t in range(turns)]

    def store(turn, t):
        cols = pl.ds(pl.multiple_of(slots[turn] * shard, shard), shard)
        return pltpu.make_async_copy(
            tile.at[turn, t], out_ref.at[pl.ds(t * height, height), cols], out_sem.at[turn, t]
        )

    for turn in range(turns):
        at = 0
        for i, n in enumerate(parts):
            if (plan[:, 2 * turn] == i).any():
                @pl.when(which[turn] == i)
                def _():
                    for j in range(n):
                        into = held.at[turn, pl.ds(j * (k // n), k // n)]
                        pltpu.make_async_copy(pieces[at + j], into, in_sem.at[turn]).start()
            at += n

    for turn in range(turns):
        @pl.when(which[turn] >= 0)
        def _():
            pltpu.make_async_copy(held.at[turn], held.at[turn], in_sem.at[turn]).wait()
            h, l = halves(held[turn])
            cat[:k] = h
            cat[k:2 * k] = h
            cat[2 * k:] = l
            for t in range(steps):
                lhs = rows_ref[t * height:(t + 1) * height, :]
                tile[turn, t] = lax.dot_general(lhs, cat[...], NN, preferred_element_type=f32)
                store(turn, t).start()

    for turn in range(turns):
        @pl.when(which[turn] >= 0)
        def _():
            for t in range(steps):
                store(turn, t).wait()


def tiles(plan, rows, pieces, out, width):
    turns = plan.shape[1] // 2
    k, shard = rows.shape[1] // 3, pieces[0][0].shape[1]
    arrays = [w for piece in pieces for w in piece]
    steps = 3 if rows.shape[0] % 48 == 0 else 2
    height = rows.shape[0] // steps
    given = [] if out is None else [out]
    return pl.pallas_call(
        functools.partial(tiles_kernel, [len(piece) for piece in pieces], plan, out is not None),
        out_shape=jax.ShapeDtypeStruct((rows.shape[0], width), f32),
        in_specs=[pl.BlockSpec(memory_space=pltpu.VMEM)] + [pl.BlockSpec(memory_space=pl.ANY)] * (len(arrays) + len(given)),
        out_specs=pl.BlockSpec(memory_space=pl.ANY),
        scratch_shapes=[
            pltpu.VMEM((turns, k, shard), f32),
            pltpu.VMEM((3 * k, shard), bf16),
            pltpu.VMEM((turns, steps, height, shard), f32),
            pltpu.SemaphoreType.DMA((turns,)),
            pltpu.SemaphoreType.DMA((turns, steps)),
        ],
        input_output_aliases={1 + len(arrays): 0} if given else {},
        compiler_params=pltpu.CompilerParams(vmem_limit_bytes=28 << 20),
        cost_estimate=pl.CostEstimate(
            flops=turns * rows.shape[0] * shard * k * 6, bytes_accessed=turns * rows.shape[0] * shard * 4, transcendentals=0
        ),
        name="tiles",
    )(rows, *arrays, *given)


def gather_all(x, n_row, n_col):
    n = n_row * n_col
    if n & (n - 1) or n_col != 2 or n < 8 or x.shape[0] % 8:
        return [lax.all_gather(x, AXES, axis=0, tiled=True)[None]], np.zeros((n, 1), np.int32)
    y, held = x[None], [0]
    bit = n // 2
    while bit > n_col:
        other = lax.ppermute(y, AXES, [(i, i ^ bit) for i in range(n)])
        y, held = jnp.concatenate([y, other]), held + [h ^ bit for h in held]
        bit //= 2
    far = lax.ppermute(y, AXES, [(i, i ^ bit) for i in range(n)])
    core = [(i, i ^ 1) for i in range(n)]
    parts = [y, far, lax.ppermute(y, AXES, core)]
    parts.append(lax.ppermute(far, AXES, core))
    spots = [h ^ flip for flip in (0, bit, 1, bit + 1) for h in held]
    return parts, np.array([[i ^ h for h in spots] for i in range(n)], np.int32)


def ring_of(mesh):
    n = mesh.shape["row"]
    at = [getattr(d, "coords", None) for d in mesh.devices[0, :, 0]]
    if any(c is None for c in at):
        return list(range(n))
    axes = [sorted({c[i] for c in at}) for i in range(3)]
    wide = [i for i in range(3) if len(axes[i]) > 1]
    index = {tuple(c): r for r, c in enumerate(at)}
    if len(wide) != 2 or len(index) != n or n != len(axes[wide[0]]) * len(axes[wide[1]]):
        return list(range(n))
    if len(axes[wide[0]]) % 2:
        wide.reverse()
    lines, places = axes[wide[0]], axes[wide[1]]

    def row(line, place):
        c = list(at[0])
        c[wide[0]], c[wide[1]] = line, place
        return index[tuple(c)]

    order = [row(lines[0], places[0])]
    for i, line in enumerate(lines):
        order += [row(line, p) for p in (places[1:] if i % 2 == 0 else places[:0:-1])]
    return order + [row(line, places[0]) for line in lines[:0:-1]]


def shards(ring, slab, predictors):
    return covariance(ring, slab, predictors)


def covariance(ring, slab, predictors):
    n_row, n_col = lax.axis_size("row"), lax.axis_size("col")
    shard, samples = slab.shape
    width = n_row * shard

    if n_col != 2 or n_row % 2 or shard % 128:
        comp, _ = basis(slab, *gather_all(predictors, n_row, n_col))
        w = lax.dot_general(slab, comp, NT, precision=lax.Precision.HIGHEST)
        every = lax.all_gather(w, AXES, axis=0, tiled=True)
        cols = lax.dynamic_slice_in_dim(every, lax.axis_index("col") * width, width)
        rows = lax.dynamic_slice_in_dim(every, lax.axis_index("row") * n_col * shard, n_col * shard)
        return jnp.dot(rows * (1.0 / samples), cols.T, precision=lax.Precision.HIGHEST)

    home = [i * n_col // n_row for i in range(n_row)]
    place = {i: p for p, i in enumerate(ring)}

    def hop(x, way, steps, source=None):
        pairs = []
        for q in range(n_row):
            a, b = ring[(q + way * (steps - 1)) % n_row], ring[(q + way * steps) % n_row]
            h = home[ring[q]]
            pairs.append((a * n_col + (h if source is None else source), b * n_col + h))
        return lax.ppermute(x, AXES, pairs)

    todo = [[[] for _ in range(n_row * n_col)], {}]

    def arrive(offset, core, w):
        key = (offset, core)
        todo[1][key] = w
        for r in range(n_row):
            for c in range(n_col):
                q = ring[(place[r] + offset) % n_row]
                if home[q] == c:
                    e = {"mine": c, "theirs": 1 - c}.get(core, core)
                    todo[0][r * n_col + c].append((key, (q - c * (n_row // n_col)) * n_col + e))

    def work(rows, out, turns=2):
        turns = min(turns, max(len(t) for t in todo[0]))
        if turns == 0:
            return out
        table, names = np.full((n_row * n_col, 2 * turns), -1, np.int32), []
        for d, waiting in enumerate(todo[0]):
            for i in range(min(turns, len(waiting))):
                key, slot = waiting.pop(0)
                if key not in names:
                    names.append(key)
                table[d, 2 * i:2 * i + 2] = names.index(key), slot
        return tiles(table, rows, [todo[1][key] for key in names], out, width)

    half = n_row // 2
    near = {}
    for way in (1, -1):
        near[way] = hop(slab, way, 1, 0)
    other = lax.ppermute(slab, "col", [(0, 1), (1, 0)])
    comp, mine = basis(slab, *gather_all(predictors, n_row, n_col))
    flights = [(1, 1, {way: hop(mine, way, 1, 1) for way in (1, -1)})]
    first = dict(zip((1, -1), project(comp, [near[1], near[-1]])))

    def onward(core, steps, sent):
        if steps + 1 < half:
            flights.append((core, steps + 1, {way: hop(sent[way], way, steps + 1) for way in sent}))
        elif steps + 1 == half:
            k = sent[1].shape[0] // 2
            flights.append((core, half, {1: hop(sent[1][:k], 1, half), -1: hop(sent[-1][k:], -1, half)}))

    onward(0, 1, first)
    rows, theirs = own_parts(comp, mine, other)
    arrive(0, "mine", [mine])
    arrive(0, "theirs", [theirs])
    for way in (1, -1):
        arrive(-way, 0, [first[way]])
    out = work(rows, None, 1)
    while flights:
        core, steps, sent = flights.pop(0)
        if steps == half and flights:
            core, steps, sent = core, half, {(c, way): w for c, _, ws in [(core, half, sent)] + flights for way, w in ws.items()}
            flights.clear()
        got = lax.optimization_barrier(tuple(sent.values()) + (out,))
        out = got[-1]
        sent = dict(zip(sent, got))
        onward(core, steps, sent)
        if steps < half:
            for way, w in sent.items():
                arrive(-way * steps, core, [w])
        else:
            for c in range(n_col):
                arrive(half, c, [sent[c, 1], sent[c, -1]])
        out = work(rows, out, (1 if steps + 1 < half else 2) if flights else 8)
    return out


def solution(mesh):
    return jax.shard_map(
        functools.partial(shards, ring_of(mesh)),
        mesh=mesh,
        in_specs=(P(("groups", "row", "col"), None), P(("groups", "row", "col"), None)),
        out_specs=P(("groups", "row"), "col"),
        check_vma=False,
    )
```

```python
import functools

import jax
import jax.numpy as jnp
import numpy as np
from jax import lax
from jax.experimental import pallas as pl
from jax.experimental.pallas import tpu as pltpu
from jax.sharding import PartitionSpec as P


f32, bf16 = jnp.float32, jnp.bfloat16
AXES = ("row", "col")
NN = (((1,), (0,)), ((), ()))
TN = (((0,), (0,)), ((), ()))
NT = (((1,), (1,)), ((), ()))


def low(a, b, dims=NN):
    return lax.dot_general(a.astype(bf16), b.astype(bf16), dims, preferred_element_type=f32)


def halves(a):
    h = a.astype(bf16)
    return h, (a - h.astype(f32)).astype(bf16)


def mid(a, b, dims=NN):
    ah, al = halves(a)
    bh, bl = halves(b)
    dot = functools.partial(lax.dot_general, dimension_numbers=dims, preferred_element_type=f32)
    return dot(ah, bh) + (dot(ah, bl) + dot(al, bh))


def high(a, b, dims=NN):
    return lax.dot_general(a, b, dims, precision=lax.Precision.HIGHEST, preferred_element_type=f32)


def eye(n):
    r = lax.broadcasted_iota(jnp.int32, (n, n), 0)
    c = lax.broadcasted_iota(jnp.int32, (n, n), 1)
    return jnp.where(r == c, 1.0, 0.0).astype(f32)


def basis_kernel(count, spots, slab_ref, *refs):
    parts, refs = refs[:count], refs[count:]
    c_ref, w_ref, x_ref, g_ref, v_ref, b_ref, z_ref, s_ref, e_ref, held, sem = refs
    m, n = x_ref.shape
    load = pltpu.make_async_copy(slab_ref, held, sem)
    load.start()
    blocks, size = parts[0].shape[:2]
    for i, part in enumerate(parts):
        for j in range(blocks):
            if count * blocks == 1:
                x_ref[...] = part[j]
            else:
                at = pick(spots[:, i * blocks + j])
                x_ref[pl.ds(pl.multiple_of(at * size, size), size), :] = part[j]
    x = x_ref[...]
    ident = eye(n)
    gram = high(x, x, TN)
    bound = jnp.max(jnp.sum(jnp.abs(gram), axis=0, keepdims=True))
    g = gram / bound
    g_ref[...] = g
    v = 3.4445 * ident - 4.7750 * g + 2.0315 * low(g, g)
    k = low(v, low(g, v))
    v = 3.4445 * v - low(v, 4.7750 * k - 2.0315 * low(k, k))
    for _ in range(2):
        k = ident - low(v, low(g, v))
        v = v + low(v, 0.5 * k + 0.375 * low(k, k))
    v_ref[...] = v

    def polish(k):
        v = v_ref[...]
        k2 = low(k, k)
        v_ref[...] = v + mid(v, 0.5 * k + 0.375 * k2 + 0.3125 * low(k, k2))

    def off(dot=high):
        v = v_ref[...]
        k = ident - dot(v, dot(g_ref[...], v), TN)
        e_ref[...] = k
        return jnp.max(jnp.abs(k))

    def again(at):
        polish(e_ref[...])
        return at[0] + 1, off()

    off(mid)
    polish(e_ref[...])
    lax.while_loop(
        lambda at: jnp.logical_and(at[0] < 60, jnp.logical_not(at[1] < 1e-4)), again, (jnp.int32(0), off())
    )
    v = v_ref[...]
    v = (v + low(v, 0.5 * e_ref[...])) * lax.rsqrt(bound)
    v_ref[...] = v
    q1 = high(x, v)
    a = q1[:n]
    s = jnp.where(jnp.sum(a * ident, axis=0, keepdims=True) < 0, 1.0, -1.0).astype(f32)
    s_ref[...] = s
    p = a.T * s
    b_ref[...] = ident - a.T * s
    z = ident + p
    for _ in range(4):
        p = low(p, p)
        z = z + low(z, p)
    z_ref[...] = z

    def refine(dot=high):
        z = z_ref[...]
        k = ident - dot(b_ref[...], z)
        z_ref[...] = z + mid(z, k + low(k, k))
        return jnp.max(jnp.abs(k))

    refine(mid)
    error = refine()

    @pl.when(jnp.logical_not(error < 3e-5))
    def _():
        e_ref[...] = q1[:n]
        rows = lax.broadcasted_iota(jnp.int32, (n, n), 0)
        cols = lax.broadcasted_iota(jnp.int32, (n, n), 1)
        lane = lax.broadcasted_iota(jnp.int32, (1, n), 1)

        def step(j, s):
            e = e_ref[...]
            row = jnp.sum(jnp.where(rows == j, e, 0.0), axis=0, keepdims=True)
            col = jnp.sum(jnp.where(cols == j, e, 0.0), axis=1, keepdims=True)
            head = jnp.sum(jnp.where(lane == j, row, 0.0), axis=1, keepdims=True)
            sign = jnp.where(head < 0, 1.0, -1.0)
            col = jnp.where(rows[:, :1] > j, col / (head - sign), 0.0)
            e_ref[...] = e - col * jnp.where(lane == j, row - sign, row)
            return jnp.where(lane == j, sign, s)

        s = lax.fori_loop(0, n, step, jnp.zeros((1, n), f32))
        s_ref[...] = s
        b = eye(n) - q1[:n].T * s
        b_ref[...] = b
        z_ref[...] = 0.49 * b.T
        lax.while_loop(
            lambda at: jnp.logical_and(at[0] < 60, jnp.logical_not(at[1] < 3e-5)),
            lambda at: (at[0] + 1, refine()),
            (jnp.int32(0), refine()),
        )
        refine()

    q2 = q1[n:]
    nt = -high(q2, z_ref[...], NT)
    c_ref[:, :n] = high(nt, a - ident * s_ref[...], NT)
    c_ref[:, n:] = eye(m - n) + high(nt, q2, NT)
    load.wait()
    ch, cl = halves(c_ref[...])
    h, l = halves(held[...])
    w_ref[...] = lax.dot_general(beside(ch, cl, ch), beside(h, h, l), NT, preferred_element_type=f32)


def basis(slab, parts, spots):
    blocks, size, n = parts[0].shape
    m = len(parts) * blocks * size
    return pl.pallas_call(
        functools.partial(basis_kernel, len(parts), spots),
        out_shape=[jax.ShapeDtypeStruct((m - n, m), f32), jax.ShapeDtypeStruct((m - n, slab.shape[0]), f32)],
        in_specs=[pl.BlockSpec(memory_space=pl.ANY)] + [pl.BlockSpec(memory_space=pltpu.VMEM)] * len(parts),
        out_specs=[pl.BlockSpec(memory_space=pltpu.VMEM)] * 2,
        scratch_shapes=[pltpu.VMEM((m, n), f32)]
        + [pltpu.VMEM((n, n), f32)] * 4
        + [pltpu.VMEM((1, n), f32), pltpu.VMEM((n, n), f32), pltpu.VMEM(slab.shape, f32), pltpu.SemaphoreType.DMA],
        compiler_params=pltpu.CompilerParams(vmem_limit_bytes=24 << 20),
        cost_estimate=pl.CostEstimate(flops=8_000_000_000, bytes_accessed=1 << 20, transcendentals=0),
        name="basis",
    )(slab, *parts)


def pick(column):
    device = lax.axis_index("row") * lax.axis_size("col") + lax.axis_index("col")
    value = jnp.int32(int(column[0]))
    for d in range(1, len(column)):
        if column[d] != column[0]:
            value = jnp.where(device == d, jnp.int32(int(column[d])), value)
    return value


def beside(*parts):
    return jnp.concatenate(parts, axis=1)


def project_kernel(count, c_ref, *refs):
    pieces, outs, (held, sem) = refs[:count], refs[count:2 * count], refs[2 * count:]
    for i in range(count):
        pltpu.make_async_copy(pieces[i], held.at[i], sem.at[i]).start()
    ch, cl = halves(c_ref[...])
    cat = beside(ch, cl, ch)
    for i in range(count):
        pltpu.make_async_copy(pieces[i], held.at[i], sem.at[i]).wait()
        h, l = halves(held[i])
        outs[i][...] = lax.dot_general(cat, beside(h, h, l), NT, preferred_element_type=f32)


def project(comp, pieces):
    count = len(pieces)
    shard, samples = pieces[0].shape
    k = comp.shape[0]
    return pl.pallas_call(
        functools.partial(project_kernel, count),
        out_shape=[jax.ShapeDtypeStruct((k, shard), f32)] * count,
        in_specs=[pl.BlockSpec(memory_space=pltpu.VMEM)] + [pl.BlockSpec(memory_space=pltpu.HBM)] * count,
        out_specs=[pl.BlockSpec(memory_space=pltpu.VMEM)] * count,
        scratch_shapes=[pltpu.VMEM((count, shard, samples), f32), pltpu.SemaphoreType.DMA((count,))],
        compiler_params=pltpu.CompilerParams(vmem_limit_bytes=24 << 20),
        cost_estimate=pl.CostEstimate(
            flops=6 * count * shard * samples * k, bytes_accessed=4 * count * shard * (samples + k), transcendentals=0
        ),
        name="project",
    )(comp, *pieces)


def own_kernel(samples, c_ref, mine_ref, theirs_ref, rows_ref, b_ref):
    core = lax.axis_index("col")
    shard = mine_ref.shape[1]
    ch, cl = halves(c_ref[...])
    h, l = halves(theirs_ref[...])
    theirs = lax.dot_general(beside(ch, cl, ch), beside(h, h, l), NT, preferred_element_type=f32)
    b_ref[...] = theirs
    for i, w in enumerate((mine_ref[...], theirs)):
        h, l = halves(w.T * (1.0 / samples))
        at = pl.ds(pl.multiple_of((core if i == 0 else 1 - core) * shard, shard), shard)
        rows_ref[at, :] = beside(h, l, h)


def own_parts(comp, mine, theirs):
    shard, samples = theirs.shape
    k = comp.shape[0]
    return pl.pallas_call(
        functools.partial(own_kernel, samples),
        out_shape=[jax.ShapeDtypeStruct((2 * shard, 3 * k), bf16), jax.ShapeDtypeStruct((k, shard), f32)],
        in_specs=[pl.BlockSpec(memory_space=pltpu.VMEM)] * 3,
        out_specs=[pl.BlockSpec(memory_space=pltpu.VMEM)] * 2,
        compiler_params=pltpu.CompilerParams(vmem_limit_bytes=24 << 20),
        cost_estimate=pl.CostEstimate(
            flops=6 * shard * samples * k, bytes_accessed=8 * shard * (samples + 2 * k), transcendentals=0
        ),
        name="own",
    )(comp, mine, theirs)


def tiles_kernel(parts, plan, given, rows_ref, *refs):
    count, turns = sum(parts), plan.shape[1] // 2
    pieces, refs = refs[:count], refs[count + (1 if given else 0):]
    out_ref, held, cat, tile, in_sem, out_sem = refs
    k, shard = held.shape[1:]
    height = tile.shape[2]
    steps = rows_ref.shape[0] // height
    which = [pick(plan[:, 2 * t]) for t in range(turns)]
    slots = [pick(plan[:, 2 * t + 1]) for t in range(turns)]

    def store(turn, t):
        cols = pl.ds(pl.multiple_of(slots[turn] * shard, shard), shard)
        return pltpu.make_async_copy(
            tile.at[turn, t], out_ref.at[pl.ds(t * height, height), cols], out_sem.at[turn, t]
        )

    for turn in range(turns):
        at = 0
        for i, n in enumerate(parts):
            if (plan[:, 2 * turn] == i).any():
                @pl.when(which[turn] == i)
                def _():
                    for j in range(n):
                        into = held.at[turn, pl.ds(j * (k // n), k // n)]
                        pltpu.make_async_copy(pieces[at + j], into, in_sem.at[turn]).start()
            at += n

    for turn in range(turns):
        @pl.when(which[turn] >= 0)
        def _():
            pltpu.make_async_copy(held.at[turn], held.at[turn], in_sem.at[turn]).wait()
            h, l = halves(held[turn])
            cat[:k] = h
            cat[k:2 * k] = h
            cat[2 * k:] = l
            for t in range(steps):
                lhs = rows_ref[t * height:(t + 1) * height, :]
                tile[turn, t] = lax.dot_general(lhs, cat[...], NN, preferred_element_type=f32)
                store(turn, t).start()

    for turn in range(turns):
        @pl.when(which[turn] >= 0)
        def _():
            for t in range(steps):
                store(turn, t).wait()


def tiles(plan, rows, pieces, out, width):
    turns = plan.shape[1] // 2
    k, shard = rows.shape[1] // 3, pieces[0][0].shape[1]
    arrays = [w for piece in pieces for w in piece]
    steps = 4 if rows.shape[0] % 64 == 0 else 2
    height = rows.shape[0] // steps
    given = [] if out is None else [out]
    return pl.pallas_call(
        functools.partial(tiles_kernel, [len(piece) for piece in pieces], plan, out is not None),
        out_shape=jax.ShapeDtypeStruct((rows.shape[0], width), f32),
        in_specs=[pl.BlockSpec(memory_space=pltpu.VMEM)] + [pl.BlockSpec(memory_space=pl.ANY)] * (len(arrays) + len(given)),
        out_specs=pl.BlockSpec(memory_space=pl.ANY),
        scratch_shapes=[
            pltpu.VMEM((turns, k, shard), f32),
            pltpu.VMEM((3 * k, shard), bf16),
            pltpu.VMEM((turns, steps, height, shard), f32),
            pltpu.SemaphoreType.DMA((turns,)),
            pltpu.SemaphoreType.DMA((turns, steps)),
        ],
        input_output_aliases={1 + len(arrays): 0} if given else {},
        compiler_params=pltpu.CompilerParams(vmem_limit_bytes=28 << 20),
        cost_estimate=pl.CostEstimate(
            flops=turns * rows.shape[0] * shard * k * 6, bytes_accessed=turns * rows.shape[0] * shard * 4, transcendentals=0
        ),
        name="tiles",
    )(rows, *arrays, *given)


def gather_all(x, n_row, n_col):
    n = n_row * n_col
    if n & (n - 1) or n_col != 2 or n < 8 or x.shape[0] % 8:
        return [lax.all_gather(x, AXES, axis=0, tiled=True)[None]], np.zeros((n, 1), np.int32)
    y, held = x[None], [0]
    bit = n // 2
    while bit > n_col:
        other = lax.ppermute(y, AXES, [(i, i ^ bit) for i in range(n)])
        y, held = jnp.concatenate([y, other]), held + [h ^ bit for h in held]
        bit //= 2
    far = lax.ppermute(y, AXES, [(i, i ^ bit) for i in range(n)])
    core = [(i, i ^ 1) for i in range(n)]
    parts = [y, far, lax.ppermute(y, AXES, core)]
    parts.append(lax.ppermute(far, AXES, core))
    spots = [h ^ flip for flip in (0, bit, 1, bit + 1) for h in held]
    return parts, np.array([[i ^ h for h in spots] for i in range(n)], np.int32)


def ring_of(mesh):
    n = mesh.shape["row"]
    at = [getattr(d, "coords", None) for d in mesh.devices[0, :, 0]]
    if any(c is None for c in at):
        return list(range(n))
    axes = [sorted({c[i] for c in at}) for i in range(3)]
    wide = [i for i in range(3) if len(axes[i]) > 1]
    index = {tuple(c): r for r, c in enumerate(at)}
    if len(wide) != 2 or len(index) != n or n != len(axes[wide[0]]) * len(axes[wide[1]]):
        return list(range(n))
    if len(axes[wide[0]]) % 2:
        wide.reverse()
    lines, places = axes[wide[0]], axes[wide[1]]

    def row(line, place):
        c = list(at[0])
        c[wide[0]], c[wide[1]] = line, place
        return index[tuple(c)]

    order = [row(lines[0], places[0])]
    for i, line in enumerate(lines):
        order += [row(line, p) for p in (places[1:] if i % 2 == 0 else places[:0:-1])]
    return order + [row(line, places[0]) for line in lines[:0:-1]]


def shards(ring, slab, predictors):
    return covariance(ring, slab, predictors)


def covariance(ring, slab, predictors):
    n_row, n_col = lax.axis_size("row"), lax.axis_size("col")
    shard, samples = slab.shape
    width = n_row * shard

    if n_col != 2 or n_row % 2 or shard % 128:
        comp, _ = basis(slab, *gather_all(predictors, n_row, n_col))
        w = lax.dot_general(slab, comp, NT, precision=lax.Precision.HIGHEST)
        every = lax.all_gather(w, AXES, axis=0, tiled=True)
        cols = lax.dynamic_slice_in_dim(every, lax.axis_index("col") * width, width)
        rows = lax.dynamic_slice_in_dim(every, lax.axis_index("row") * n_col * shard, n_col * shard)
        return jnp.dot(rows * (1.0 / samples), cols.T, precision=lax.Precision.HIGHEST)

    home = [i * n_col // n_row for i in range(n_row)]
    place = {i: p for p, i in enumerate(ring)}

    def hop(x, way, steps, source=None):
        pairs = []
        for q in range(n_row):
            a, b = ring[(q + way * (steps - 1)) % n_row], ring[(q + way * steps) % n_row]
            h = home[ring[q]]
            pairs.append((a * n_col + (h if source is None else source), b * n_col + h))
        return lax.ppermute(x, AXES, pairs)

    todo = [[[] for _ in range(n_row * n_col)], {}]

    def arrive(offset, core, w):
        key = (offset, core)
        todo[1][key] = w
        for r in range(n_row):
            for c in range(n_col):
                q = ring[(place[r] + offset) % n_row]
                if home[q] == c:
                    e = {"mine": c, "theirs": 1 - c}.get(core, core)
                    todo[0][r * n_col + c].append((key, (q - c * (n_row // n_col)) * n_col + e))

    def work(rows, out, turns=2):
        turns = min(turns, max(len(t) for t in todo[0]))
        if turns == 0:
            return out
        table, names = np.full((n_row * n_col, 2 * turns), -1, np.int32), []
        for d, waiting in enumerate(todo[0]):
            for i in range(min(turns, len(waiting))):
                key, slot = waiting.pop(0)
                if key not in names:
                    names.append(key)
                table[d, 2 * i:2 * i + 2] = names.index(key), slot
        return tiles(table, rows, [todo[1][key] for key in names], out, width)

    half = n_row // 2
    near = {}
    for way in (1, -1):
        near[way] = hop(slab, way, 1, 0)
    other = lax.ppermute(slab, "col", [(0, 1), (1, 0)])
    comp, mine = basis(slab, *gather_all(predictors, n_row, n_col))
    flights = [(1, 1, {way: hop(mine, way, 1, 1) for way in (1, -1)})]
    first = dict(zip((1, -1), project(comp, [near[1], near[-1]])))

    def onward(core, steps, sent):
        if steps + 1 < half:
            flights.append((core, steps + 1, {way: hop(sent[way], way, steps + 1) for way in sent}))
        elif steps + 1 == half:
            way = (1, -1)[core]
            flights.append((core, half, {way: hop(sent[way], way, half)}))

    onward(0, 1, first)
    rows, theirs = own_parts(comp, mine, other)
    arrive(0, "mine", [mine])
    arrive(0, "theirs", [theirs])
    for way in (1, -1):
        arrive(-way, 0, [first[way]])
    out = None
    while flights:
        core, steps, sent = flights.pop(0)
        needed = [(1, -1)[core]] if steps + 1 == half else list(sent)
        got = lax.optimization_barrier(tuple(sent[way] for way in needed) + (rows if out is None else out,))
        turns = 1 if steps + 1 < half and out is not None else 2
        rows, out = (got[-1], None) if out is None else (rows, got[-1])
        sent.update(zip(needed, got))
        onward(core, steps, sent)
        for way, w in sent.items():
            arrive(half if steps == half else -way * steps, core, [w])
        out = work(rows, out, turns if flights else 8)
    return out


def solution(mesh):
    return jax.shard_map(
        functools.partial(shards, ring_of(mesh)),
        mesh=mesh,
        in_specs=(P(("groups", "row", "col"), None), P(("groups", "row", "col"), None)),
        out_specs=P(("groups", "row"), "col"),
        check_vma=False,
    )
```
